256 devices in a mesh: segment: 4 (over z_hi, core), dp: 16 (over z_lo, y), mp: 4 (over x).
Axes of the slice: x: 4, y: 4, z: 8 (z_hi: 2, z_lo: 4; z = z_hi * 4 + z_lo), core: 2. Of those that a mesh axis runs over, the one named last changes fastest.
Arguments:
- hidden: bfloat16 [384, 64, 4096], P(('segment', 'dp'))
- final_gain: bfloat16 [4096], replicated, may hold values from 0.099609375 to 1.8984375
- key_weight: bfloat16 [4096, 2048], P('dp', 'mp'), may hold values from -0.09375 to 0.09375
- value_weight: bfloat16 [4096, 2048], P('dp', 'mp'), may hold values from -0.09375 to 0.09375
- queries: bfloat16 [32, 128, 2048], P('dp', None, 'mp'), may hold values from -6 to 6
- context_grad: bfloat16 [32, 128, 2048], P('dp', None, 'mp'), may hold values from -384 to 384
- passage_count: int32 [32], replicated, may hold values from 4 to 16, as said below
- passage_slot: int32 [32, 16], replicated, may hold values from -1 to 287, as said below
- slot_question: int32 [32], replicated, may hold values from 0 to 31, as said below
Outputs:
- grad_hidden: bfloat16 [384, 64, 4096], P(('segment', 'dp'), 'mp')
The draws below stay inside these ranges and needn't reach their ends.
Inputs may be any that keep to these rules, and one draw needn't show every extreme that they name: `passage_count`: the counts add up to 288, and some question has 16 passages. `passage_slot`: entry [q, j] is the slot holding passage j of question q for j below passage_count[q], and -1 beyond. Slots are numbered device by device in the order of the segment and dp indices, 6 to a device; only devices of the first three segment indices hold passages, each of their slots exactly one, and no slot is named twice. One device holds at most 1 passages of the questions served by the decoder rows of one dp index (rows 2 * c to 2 * c + 1 on dp index c), and one segment index at most 6 passages of one question; both bounds are reached. `slot_question`: A permutation.
All inputs are finite; a program needn't handle non-finite values.
Results may differ from the reference program's by a relative error of at most 0.015.
Values may be sent and summed in bfloat16 or wider, within the bound.
A program may use at most 128 MiB of HBM per device.

```python
import math
import jax
import jax.numpy as jnp
from jax import lax

D = 4096
HEADS = 32
HEAD_DIM = 64
INNER = 2048
LEN = 64
TGT = 128
MAXP = 16
MINP = 4
PAVG = 9
P_DEV = 6
Q = 32
ES = 384
N_SEGMENT = 4
N_DP = 16
N_MP = 4


def draw_hidden(key, part):
    base_key = jax.random.fold_in(key, 101)
    value_key, row_key, col_key = jax.random.split(base_key, 3)
    full_shape = (ES, LEN, D)
    col_scale = jnp.exp(jax.random.uniform(col_key, (1, 1, D), jnp.float32, math.log(0.3), math.log(3.0)))
    row_scale = jnp.exp(jax.random.uniform(row_key, (ES, LEN, 1), jnp.float32, math.log(0.5), math.log(5.0)))
    values = jax.random.normal(value_key, full_shape, jnp.float32)
    return (values * row_scale * col_scale).astype(jnp.bfloat16)


def shuffle_slots(slot_key):
    return jax.random.permutation(slot_key, P_DEV).astype(jnp.int32)


def deal_passages(key):
    base_key = jax.random.fold_in(key, 7919)
    full_key, add_key, order_key, column_key, slot_key, turn_key = jax.random.split(base_key, 6)
    question_ids = jnp.arange(Q, dtype=jnp.int32)
    chosen = jax.random.randint(full_key, (), 0, Q, dtype=jnp.int32)
    counts = jnp.where(question_ids == chosen, MAXP, MINP).astype(jnp.int32)
    spare_units = PAVG * Q - MAXP - MINP * (Q - 1)

    def add_one(step_no, counts):
        begin_at = jax.random.randint(jax.random.fold_in(add_key, step_no), (), 0, Q, dtype=jnp.int32)
        distance = (question_ids - begin_at) % Q + Q * (counts >= MAXP).astype(jnp.int32)
        picked = jnp.argmin(distance).astype(jnp.int32)
        return counts + (question_ids == picked).astype(jnp.int32)
    counts = lax.fori_loop(0, spare_units, add_one, counts)
    row_question = jax.random.permutation(order_key, Q).astype(jnp.int32)
    ordered = counts[row_question]
    begins = (jnp.cumsum(ordered) - ordered).astype(jnp.int32)
    offsets = jnp.zeros((Q,), jnp.int32).at[row_question].set(begins)
    encoders = (N_SEGMENT - 1) * N_DP
    capacity = P_DEV * encoders
    turn = jax.random.randint(turn_key, (), 0, capacity, dtype=jnp.int32)
    serial = (offsets[:, None] + jnp.arange(MAXP, dtype=jnp.int32)[None, :] + turn) % capacity
    device = serial % encoders
    round_no = serial // encoders
    column_perm = jax.random.permutation(column_key, N_DP).astype(jnp.int32)
    segment_no = device % (N_SEGMENT - 1)
    column_no = column_perm[device // (N_SEGMENT - 1)]
    slot_orders = jax.vmap(shuffle_slots)(jax.random.split(slot_key, encoders))
    slot_no = slot_orders[device, round_no]
    global_slot = (segment_no * N_DP + column_no) * P_DEV + slot_no
    live_entry = jnp.arange(MAXP, dtype=jnp.int32)[None, :] < counts[:, None]
    return (counts, jnp.where(live_entry, global_slot, -1).astype(jnp.int32), row_question)


def draw_passage_count(key, part):
    return deal_passages(key)[0]


def draw_passage_slot(key, part):
    return deal_passages(key)[1]


def draw_slot_question(key, part):
    return deal_passages(key)[2]


def steps_of(key, extent, cuts, least, high):
    factor_of, own = 1.0, jax.random.fold_in(key, 6)
    for axis_at, shards_of in cuts:
        draws = jnp.exp(jax.random.uniform(jax.random.fold_in(own, axis_at), (shards_of,), jnp.float32, least / len(cuts), high / len(cuts)))
        factor_of = factor_of * jnp.repeat(draws, extent[axis_at] // shards_of).reshape([-1 if axis == axis_at else 1 for axis in range(len(extent))])
    return factor_of


def scatter_about(own_key, dims, deviation, bound, pieces=(), kind=jnp.bfloat16):
    level = steps_of(own_key, dims, pieces, -0.22, 0.18) if pieces else 1.0
    array = jax.random.normal(own_key, dims, jnp.float32) * deviation * level
    return jnp.minimum(jnp.maximum(array, -bound), bound).astype(kind)


def setup_inputs(seed: int = 0) -> dict:
    streams_of = jax.random.split(jax.random.key(seed), 10)
    return {
        "hidden": draw_hidden(jax.random.fold_in(streams_of[9], 71), 0),
        "final_gain": jnp.clip(1.0 + 0.18 * jax.random.normal(streams_of[1], (D,), jnp.float32), 0.099609375, 1.8984375).astype(jnp.bfloat16),
        "key_weight": scatter_about(streams_of[2], (D, INNER), D ** -0.5, 0.09375, ((0, 16), (1, 4))),
        "value_weight": scatter_about(streams_of[3], (D, INNER), D ** -0.5, 0.09375, ((0, 16), (1, 4))),
        "queries": scatter_about(streams_of[4], (Q, TGT, INNER), 1.0, 6.0, ((0, 16), (2, 4))),
        "context_grad": scatter_about(streams_of[5], (Q, TGT, INNER), 64.0, 384.0, ((0, 16), (2, 4))),
        "passage_count": draw_passage_count(jax.random.fold_in(streams_of[9], 71), 0),
        "passage_slot": draw_passage_slot(jax.random.fold_in(streams_of[9], 71), 0),
        "slot_question": draw_slot_question(jax.random.fold_in(streams_of[9], 71), 0),
    }


EPSILON = 1e-06

def reference(hidden, final_gain, key_weight, value_weight, queries, context_grad, passage_count, passage_slot, slot_question):
    scaling = 1.0 / math.sqrt(HEAD_DIM)
    group_width = INNER // N_MP
    positions = jnp.arange(Q, dtype=jnp.int32)
    home_row = jnp.zeros((Q,), jnp.int32).at[slot_question].set(positions)
    gain_vec = final_gain.astype(jnp.float32)
    passage_ids = jnp.arange(MAXP, dtype=jnp.int32)

    def per_question(question):
        slot_ids = passage_slot[question]
        present = (slot_ids >= 0) & (passage_ids < passage_count[question])
        safe_ids = jnp.where(present, slot_ids, 0).astype(jnp.int32)
        states = hidden[safe_ids].astype(jnp.float32)
        inv_rms = lax.rsqrt(lax.optimization_barrier(jnp.mean(states * states, axis=-1, keepdims=True)) + EPSILON)
        normed = (states * inv_rms * gain_vec).astype(jnp.bfloat16).reshape(MAXP * LEN, D)
        key_rows = jnp.dot(normed, key_weight, preferred_element_type=jnp.float32).astype(jnp.bfloat16)
        value_rows = jnp.dot(normed, value_weight, preferred_element_type=jnp.float32).astype(jnp.bfloat16)
        decoder_row = home_row[question]
        query_heads = queries[decoder_row].astype(jnp.float32).reshape(TGT, HEADS, HEAD_DIM)
        grad_heads = context_grad[decoder_row].astype(jnp.float32).reshape(TGT, HEADS, HEAD_DIM)
        key_heads = key_rows.astype(jnp.float32).reshape(MAXP * LEN, HEADS, HEAD_DIM)
        value_heads = value_rows.astype(jnp.float32).reshape(MAXP * LEN, HEADS, HEAD_DIM)
        scores = jnp.einsum('thd,khd->htk', query_heads, key_heads) * scaling
        live_keys = jnp.repeat(present, LEN).astype(jnp.float32)
        weights = jnp.exp(scores) * live_keys[None, None, :]
        attn_probs = weights / lax.optimization_barrier(jnp.sum(weights, axis=-1, keepdims=True))
        probs_half = attn_probs.astype(jnp.bfloat16)
        context = jnp.einsum('htk,khd->thd', probs_half.astype(jnp.float32), value_heads).astype(jnp.bfloat16)
        row_delta = lax.optimization_barrier(jnp.sum(grad_heads * context.astype(jnp.float32), axis=-1))
        prob_grads = jnp.einsum('thd,khd->htk', grad_heads, value_heads)
        score_grads = (attn_probs * (prob_grads - row_delta.T[:, :, None])).astype(jnp.bfloat16)
        key_grads = (jnp.einsum('htk,thd->khd', score_grads.astype(jnp.float32), query_heads) * scaling).astype(jnp.bfloat16)
        value_grads = jnp.einsum('htk,thd->khd', probs_half.astype(jnp.float32), grad_heads).astype(jnp.bfloat16)
        key_grads = key_grads.reshape(MAXP * LEN, INNER)
        value_grads = value_grads.reshape(MAXP * LEN, INNER)
        normed_grad = jnp.zeros((MAXP * LEN, D), jnp.float32)
        for group_no in range(N_MP):
            first_col = group_no * group_width
            last_col = first_col + group_width
            group_term = jnp.dot(key_grads[:, first_col:last_col], key_weight[:, first_col:last_col].T, preferred_element_type=jnp.float32)
            group_term = group_term + jnp.dot(value_grads[:, first_col:last_col], value_weight[:, first_col:last_col].T, preferred_element_type=jnp.float32)
            term_half = lax.optimization_barrier(group_term.astype(jnp.bfloat16))
            normed_grad = normed_grad + term_half.astype(jnp.float32)
        scaled = gain_vec * normed_grad.reshape(MAXP, LEN, D)
        hidden_grads = inv_rms * scaled - states * inv_rms ** 3 * lax.optimization_barrier(jnp.mean(states * scaled, axis=-1, keepdims=True))
        targets = jnp.where(present, slot_ids, ES).astype(jnp.int32)
        return (hidden_grads.astype(jnp.bfloat16), targets)
    hidden_grads, targets = lax.map(per_question, positions)
    output = jnp.zeros((ES, LEN, D), jnp.bfloat16)
    return output.at[targets.reshape(-1)].set(hidden_grads.reshape(Q * MAXP, LEN, D), mode='drop')
```

```python
import functools
import math

import jax
import jax.numpy as jnp
from jax import lax
from jax.experimental import pallas as pl
from jax.experimental.pallas import tpu as pltpu
from jax.sharding import PartitionSpec as P

HEAD_DIM = 64
EPSILON = 1e-06
TINY = 1.2e-38
MESH = pl.DeviceIdType.MESH

ARRIVAL = (
    (3, 0), (1, 0), (0, 3), (0, 1), (2, 0), (3, 3), (3, 1), (1, 3), (1, 1), (0, 2), (2, 3), (2, 1), (3, 2), (1, 2), (2, 2),
)
FIRST_TABLE = sum(first * 4**k for k, (first, _) in enumerate(ARRIVAL))
SECOND_TABLE = sum(second * 4**k for k, (_, second) in enumerate(ARRIVAL))
OTHERS = len(ARRIVAL)
LAG = 2


def reader_kernel(
    owner, counts, slots, gain, hidden_hbm, key_shard, value_shard, query_shard, grad_shard,
    out,
    blocks, states, normed, total, kv_rows, score_buf, prob_grad_buf, stats, grad_rows, send_buf, recv_buf, sum_buf,
    local_sem, first_send, second_send, mate_send, block_recv, mate_recv,
    stat_send_y, stat_recv_y, stat_send_z, stat_recv_z, stat_send_mate, stat_recv_mate,
    ring_send, ring_recv,
):
    segment, column, x = lax.axis_index("segment"), lax.axis_index("dp"), lax.axis_index("mp")
    z_hi, core = lax.div(segment, 2), lax.rem(segment, 2)
    z_lo, y = lax.div(column, 4), lax.rem(column, 4)
    z_next, z_prev = lax.rem(z_lo + 1, 4), lax.rem(z_lo + 3, 4)
    flip_next, flip_prev = lax.div(z_lo + 1, 4), 1 - lax.div(z_lo + 3, 4)
    y_up = (segment, z_lo * 4 + lax.rem(y + 1, 4), x)
    y_down = (segment, z_lo * 4 + lax.rem(y + 3, 4), x)
    z_up = (lax.rem(z_hi + flip_next, 2) * 2 + core, z_next * 4 + y, x)
    z_down = (lax.rem(z_hi + flip_prev, 2) * 2 + core, z_prev * 4 + y, x)
    mate = (z_hi * 2 + 1 - core, column, x)
    x_up = (segment, column, lax.rem(x + 1, 4))
    x_down = (segment, column, lax.rem(x + 3, 4))

    def by_core(if_zero, if_one):
        return tuple(a * (1 - core) + b * core for a, b in zip(if_zero, if_one))

    first_up, first_down = by_core(y_up, z_up), by_core(y_down, z_down)
    second_up, second_down = by_core(z_up, y_up), by_core(z_down, y_down)
    first_at = y * (1 - core) + z_lo * core
    second_at = z_lo * (1 - core) + y * core
    first_stride, second_stride = 1 + 3 * core, 4 - 3 * core
    other = 1 - core

    def remote(src, dst, send, recv, device):
        return pltpu.make_async_remote_copy(
            src_ref=src, dst_ref=dst, send_sem=send, recv_sem=recv, device_id=device, device_id_type=MESH
        )

    mine = pl.ds(2 * column, 2)
    local_copies = [
        pltpu.make_async_copy(src, dst, local_sem.at[k])
        for k, (src, dst) in enumerate(
            (
                (key_shard, blocks.at[0, 0, mine]),
                (value_shard, blocks.at[0, 1, mine]),
                (query_shard, blocks.at[1, 0, mine]),
                (grad_shard, blocks.at[1, 1, mine]),
                (hidden_hbm, states),
            )
        )
    ]
    for copy in local_copies:
        copy.start()
    barrier = pltpu.get_barrier_semaphore()
    for device in (y_up, y_down, z_up, z_down, mate, x_up, x_down):
        pl.semaphore_signal(barrier, inc=1, device_id=device, device_id_type=MESH)
    pl.semaphore_wait(barrier, 7)
    for copy in local_copies[:4]:
        copy.wait()

    def block_copy(kind, index, send, recv, device):
        ref = blocks.at[kind, core, index]
        return remote(ref, ref, send, recv, device)

    def to_first(kind, way, which, index):
        return block_copy(
            kind, index, first_send.at[kind, way, which], block_recv.at[kind, index], (first_up, first_down)[way]
        )

    def to_second(kind, lane, way, which, index):
        return block_copy(
            kind, index, second_send.at[kind, lane, way, which], block_recv.at[kind, index],
            (second_up, second_down)[way],
        )

    def to_mate(kind, index):
        return block_copy(kind, index, mate_send.at[kind, index], mate_recv.at[kind, index], mate)

    def send_own(kind):
        for half in range(2):
            for way in range(2):
                to_first(kind, way, half, 2 * column + half).start()
        for half in range(2):
            for way in range(2):
                to_second(kind, 0, way, half, 2 * column + half).start()

    send_own(0)
    local_copies[4].wait()

    slots_here = states.shape[0]
    width = states.shape[-1]
    parts = states.shape[1]
    token_share = states.shape[2]

    def norm_rows(step, carry):
        slot, part = lax.div(step, parts), lax.rem(step, parts)
        rows = states[slot, part].astype(jnp.float32)
        inv = lax.rsqrt(jnp.mean(rows * rows, axis=-1, keepdims=True) + EPSILON)
        scaled = (rows * inv * gain[...]).astype(jnp.bfloat16)
        at = pl.ds(pl.multiple_of(step * token_share, token_share), token_share)
        for shard in range(16):
            normed[shard, at, :] = scaled[:, shard * 256 : shard * 256 + 256]
        return carry

    lax.fori_loop(0, slots_here * parts, norm_rows, 0)

    def project(which, shard, first):
        weight = blocks[0, which, pl.ds(2 * shard, 2)].reshape(256, blocks.shape[-1])
        product = jnp.dot(normed[shard], weight, preferred_element_type=jnp.float32)
        total[which] = product if first else total[which] + product

    project(0, column, True)
    project(1, column, True)

    def table(power, first_base, second_base, stride_first, stride_second):
        first, second = lax.rem(lax.div(FIRST_TABLE, power), 4), lax.rem(lax.div(SECOND_TABLE, power), 4)
        shard = lax.rem(first_base + first, 4) * stride_first + lax.rem(second_base + second, 4) * stride_second
        return first, second, shard

    def next_power(power, k):
        return jnp.where(k == OTHERS - 1, 1, power * 4)

    def gather_step(step, powers):
        power, mate_power = powers
        kind, k = lax.div(step, OTHERS), lax.rem(step, OTHERS)

        @pl.when(step < 2 * OTHERS)
        def _():
            first, second, shard = table(power, first_at, second_at, first_stride, second_stride)
            for half in range(2):
                index = 2 * shard + half
                to_first(kind, 0, 0, index).wait_recv()

                @pl.when(second == 0)
                def _():
                    to_second(kind, first, 0, half, index).start()
                    to_second(kind, first, 1, half, index).start()

                @pl.when((second == 0) & (first == (3 if half == 0 else 1)))
                def _():
                    to_first(kind, half, 2, index).start()

                @pl.when(second == (3 if half == 0 else 1))
                def _():
                    to_second(kind, first, half, 2, index).start()

                to_mate(kind, index).start()

            @pl.when(kind == 0)
            def _():
                project(core, shard, False)

        @pl.when(step == OTHERS - 6)
        def _():
            send_own(1)

        back = step - LAG

        @pl.when(back >= 0)
        def _():
            mate_kind = lax.div(back, OTHERS)
            _, _, shard = table(mate_power, second_at, first_at, second_stride, first_stride)
            for half in range(2):
                ref = blocks.at[mate_kind, other, 2 * shard + half]
                remote(
                    ref, ref, mate_send.at[mate_kind, 2 * shard + half], mate_recv.at[mate_kind, 2 * shard + half], mate
                ).wait_recv()

            @pl.when(mate_kind == 0)
            def _():
                project(other, shard, False)

        new_mate = jnp.where(back >= 0, next_power(mate_power, lax.rem(jnp.maximum(back, 0), OTHERS)), mate_power)
        return next_power(power, k), new_mate

    lax.fori_loop(0, 2 * OTHERS + LAG, gather_step, (jnp.int32(1), jnp.int32(1)))

    for which in range(2):
        for slot in range(slots_here):
            kv_rows[which, slot] = total[which, slot * 64 : slot * 64 + 64, :].astype(jnp.bfloat16)

    lane = lax.broadcasted_iota(jnp.int32, (64, 128), 1)
    left = lane < HEAD_DIM
    left_half = left.astype(jnp.float32).astype(jnp.bfloat16)
    right_half = (1.0 - left.astype(jnp.float32)).astype(jnp.bfloat16)
    pairs = kv_rows.shape[-1] // 128
    scaling = 1.0 / math.sqrt(HEAD_DIM)
    across = (((1,), (1,)), ((), ()))

    def both_heads(top, bottom):
        return jnp.concatenate([jnp.broadcast_to(top, (64, 128)), jnp.broadcast_to(bottom, (64, 128))], axis=0)

    me = segment * 16 + column

    def scores_of(slot, carry):
        row = owner[slots_here + slot]
        sums, deltas = [], []
        for pair in range(pairs):
            cols = slice(pair * 128, pair * 128 + 128)
            keys, values = kv_rows[0, slot, :, cols], kv_rows[1, slot, :, cols]
            key_pair = jnp.concatenate([keys * left_half, keys * right_half], axis=0)
            value_pair = jnp.concatenate([values * left_half, values * right_half], axis=0)
            queries = blocks[1, 0, row, :, cols]
            grads = blocks[1, 1, row, :, cols]
            scores = lax.dot_general(key_pair, queries, across, preferred_element_type=jnp.float32) * scaling
            prob_grads = lax.dot_general(value_pair, grads, across, preferred_element_type=jnp.float32)
            score_buf[slot, pair] = scores
            prob_grad_buf[slot, pair] = prob_grads
            weights = jnp.exp(scores)
            both = [jnp.sum(weights[k * 64 : k * 64 + 64], axis=0, keepdims=True) for k in range(2)]
            log_both = both_heads(*[jnp.log(jnp.maximum(b, TINY)) for b in both])
            moved = jnp.exp(scores - log_both) * prob_grads
            sums += both
            deltas += [jnp.sum(moved[k * 64 : k * 64 + 64], axis=0, keepdims=True) for k in range(2)]
        stats[me, slot] = jnp.concatenate(sums + deltas, axis=0).astype(jnp.bfloat16)
        return carry

    lax.fori_loop(0, slots_here, scores_of, 0)

    z = z_hi * 4 + z_lo
    half_slots = slots_here // 2
    halves = (pl.ds(0, half_slots), pl.ds(half_slots, half_slots))
    whole = pl.ds(0, slots_here)

    def piece(z_of, y_of, core_of):
        return (lax.div(z_of, 4) * 2 + core_of) * 16 + lax.rem(z_of, 4) * 4 + y_of

    def stat_copy(at, part, send, recv, device):
        ref = stats.at[at, part]
        return remote(ref, ref, send, recv, device)

    def y_piece(offset):
        return piece(z, lax.rem(y + offset, 4), core)

    def along_y(way, which, offset, part):
        return stat_copy(
            y_piece(offset), part, stat_send_y.at[way, which], stat_recv_y.at[way, which], (y_up, y_down)[way]
        )

    def share(z_of, y_of, part, which):
        at = piece(z_of, y_of, core)
        return stat_copy(
            at, part, stat_send_mate.at[z_of * 4 + y_of, which], stat_recv_mate.at[z_of * 4 + y_of, which], mate
        )

    def along_z(way, lane_y, distance, part):
        z_of = lax.rem(z + (8 - distance if way == 0 else distance), 8)
        at = piece(z_of, lax.rem(y + lane_y, 4), core)
        return stat_copy(
            at, part, stat_send_z.at[way, lane_y, distance], stat_recv_z.at[way, lane_y, distance],
            (z_up, z_down)[way],
        )

    along_y(0, 0, 0, whole).start()
    along_y(1, 0, 0, whole).start()
    along_z(0, 0, 0, whole).start()
    along_z(1, 0, 0, whole).start()
    share(z, y, whole, 0).start()
    for way, offset in ((0, 3), (1, 1)):
        along_y(way, 0, offset, whole).wait_recv()
        along_y(way, 1, offset, halves[way]).start()
        along_z(0, offset, 0, whole).start()
        along_z(1, offset, 0, whole).start()
        share(z, lax.rem(y + offset, 4), whole, 0).start()
    for way in range(2):
        along_y(way, 1, 2, halves[way]).wait_recv()
    along_z(0, 2, 0, whole).start()
    along_z(1, 2, 0, whole).start()
    share(z, lax.rem(y + 2, 4), whole, 0).start()
    for distance in (1, 2, 3, 4):
        for lane_y in (0, 3, 1, 2):
            y_of = lax.rem(y + lane_y, 4)
            for way in range(2):
                z_of = lax.rem(z + (8 - distance if way == 0 else distance), 8)
                along_z(way, lane_y, distance - 1, halves[way] if distance == 4 else whole).wait_recv()
                if distance < 4:
                    along_z(way, lane_y, distance, halves[way] if distance == 3 else whole).start()
                    share(z_of, y_of, whole, 0).start()
                else:
                    share(z_of, y_of, halves[way], way).start()

    def mate_stats(fn):
        def step(k, carry):
            z_of, y_of = lax.div(k, 4), lax.rem(k, 4)
            fn(z_of, y_of)
            return carry

        lax.fori_loop(0, 32, step, 0)

    def wait_mate(z_of, y_of, received):
        far = lax.rem(z_of - z + 8, 8) == 4

        def finish(copy):
            copy.wait_recv() if received else copy.wait_send()

        @pl.when(far)
        def _():
            for way in range(2):
                finish(share(z_of, y_of, halves[way], way))

        @pl.when(jnp.logical_not(far))
        def _():
            finish(share(z_of, y_of, whole, 0))

    mate_stats(functools.partial(wait_mate, received=True))

    def grads_of(slot, carry):
        question = owner[slot]
        row = owner[slots_here + slot]
        holds = question >= 0
        base = jnp.maximum(question, 0)
        count = counts[base]
        tiles = []
        for k in range(16):
            at = slots[base * 16 + k]
            tile = stats[lax.div(at, slots_here), lax.rem(at, slots_here)].astype(jnp.float32)
            tiles.append((tile[:8], tile[8:], k < count))
        zero = jnp.zeros((8, 128), jnp.float32)
        all_sum = zero
        for sums, _, live in tiles:
            all_sum = all_sum + jnp.where(live, sums, zero)
        log_sum = jnp.log(jnp.maximum(all_sum, TINY))
        delta = zero
        for sums, deltas, live in tiles:
            share_of = jnp.exp(jnp.log(jnp.maximum(sums, TINY)) - log_sum)
            delta = delta + jnp.where(live, share_of * deltas, zero)
        at = pl.ds(pl.multiple_of(slot * token_share, token_share), token_share)
        inner = kv_rows.shape[-1]
        for pair in range(pairs):
            cols = slice(pair * 128, pair * 128 + 128)
            heads = [2 * pair, 2 * pair + 1]
            log_both = both_heads(*[log_sum[h : h + 1] for h in heads])
            delta_both = both_heads(*[delta[h : h + 1] for h in heads])
            probs = jnp.exp(score_buf[slot, pair] - log_both)
            score_grads = (probs * (prob_grad_buf[slot, pair] - delta_both)).astype(jnp.bfloat16)
            queries = blocks[1, 0, row, :, cols]
            grads = blocks[1, 1, row, :, cols]
            key_grads = jnp.dot(score_grads, queries, preferred_element_type=jnp.float32) * scaling
            value_grads = jnp.dot(probs.astype(jnp.bfloat16), grads, preferred_element_type=jnp.float32)
            for offset, both in ((0, key_grads), (inner, value_grads)):
                merged = jnp.where(left, both[:64], both[64:])
                merged = jnp.where(holds, merged, jnp.zeros_like(merged)).astype(jnp.bfloat16)
                for part in range(parts):
                    grad_rows[part, at, offset + pair * 128 : offset + pair * 128 + 128] = merged[
                        part * token_share : part * token_share + token_share
                    ]
        return carry

    lax.fori_loop(0, slots_here, grads_of, 0)

    rows_half = slots_here * token_share // 2
    chunks = recv_buf.shape[2]
    chunk_width = recv_buf.shape[-1]
    tiles_here = chunk_width // 256

    def lhs(first, second):
        return jnp.concatenate([grad_rows[first], grad_rows[second]], axis=0)

    def back(rows, chunk, tile):
        index = pl.ds(2 * (chunk * tiles_here + tile), 2)
        inner = kv_rows.shape[-1]
        keys = blocks[0, 0, index].reshape(256, inner)
        values = blocks[0, 1, index].reshape(256, inner)
        return lax.dot_general(rows[:, :inner], keys, across, preferred_element_type=jnp.float32) + lax.dot_general(
            rows[:, inner:], values, across, preferred_element_type=jnp.float32
        )

    def ring(step, way, chunk):
        return remote(
            send_buf.at[step, way, chunk], recv_buf.at[step, way, chunk],
            ring_send.at[step, way, chunk], ring_recv.at[step, way, chunk], (x_up, x_down)[way],
        )

    def first_chunk(chunk, carry):
        rows = lhs(lax.rem(x + 3, 4), lax.rem(x + 1, 4))
        for tile in range(tiles_here):
            cols = slice(tile * 256, tile * 256 + 256)
            product = back(rows, chunk, tile).astype(jnp.bfloat16)
            send_buf[0, 0, chunk, :, cols] = product[:rows_half]
            send_buf[2, 1, chunk, :, cols] = product[rows_half : 2 * rows_half]
            send_buf[2, 0, chunk, :, cols] = product[2 * rows_half : 3 * rows_half]
            send_buf[0, 1, chunk, :, cols] = product[3 * rows_half :]
        ring(0, 0, chunk).start()
        ring(0, 1, chunk).start()
        return carry

    lax.fori_loop(0, chunks, first_chunk, 0)

    def pass_on(step, chunk):
        for way in range(2):
            ring(step - 1, way, chunk).wait_recv()
            send_buf[step, way, chunk] = (
                send_buf[step, way, chunk].astype(jnp.float32) + recv_buf[step - 1, way, chunk].astype(jnp.float32)
            ).astype(jnp.bfloat16)
            ring(step, way, chunk).start()

    def second_chunk(chunk, carry):
        rows = lhs(lax.rem(x + 2, 4), x)
        for tile in range(tiles_here):
            cols = slice(tile * 256, tile * 256 + 256)
            product = back(rows, chunk, tile).astype(jnp.bfloat16)
            send_buf[1, 0, chunk, :, cols] = product[:rows_half]
            send_buf[1, 1, chunk, :, cols] = product[rows_half : 2 * rows_half]
            sum_buf[chunk, :, cols] = product[2 * rows_half :].astype(jnp.float32)
        pass_on(1, chunk)
        return carry

    lax.fori_loop(0, chunks, second_chunk, 0)

    def third_chunk(chunk, carry):
        pass_on(2, chunk)
        return carry

    lax.fori_loop(0, chunks, third_chunk, 0)

    def last_chunk(chunk, carry):
        for way in range(2):
            ring(2, way, chunk).wait_recv()
            at = slice(way * rows_half, way * rows_half + rows_half)
            sum_buf[chunk, at] = sum_buf[chunk, at] + recv_buf[2, way, chunk].astype(jnp.float32)
        return carry

    lax.fori_loop(0, chunks, last_chunk, 0)

    def finish_slot(slot, carry):
        at = pl.ds(pl.multiple_of(slot * token_share, token_share), token_share)
        rows = states[slot, x].astype(jnp.float32)
        inv = lax.rsqrt(jnp.mean(rows * rows, axis=-1, keepdims=True) + EPSILON)
        scaled = gain[...] * jnp.concatenate([sum_buf[c, at, :] for c in range(chunks)], axis=-1)
        mean = jnp.mean(rows * scaled, axis=-1, keepdims=True)
        out[slot] = (inv * scaled - rows * (inv * inv * inv) * mean).astype(jnp.bfloat16)
        return carry

    lax.fori_loop(0, slots_here, finish_slot, 0)

    for kind in range(2):
        for way in range(2):
            for which in range(3):
                to_first(kind, way, which, 2 * column).wait_send()

    def drain_second(k, carry):
        for kind in range(2):
            for way in range(2):
                for which in range(3):
                    to_second(kind, k, way, which, 2 * column).wait_send()
        return carry

    lax.fori_loop(0, 4, drain_second, 0)

    def drain_mate(k, power):
        _, _, shard = table(power, first_at, second_at, first_stride, second_stride)
        for kind in range(2):
            for half in range(2):
                to_mate(kind, 2 * shard + half).wait_send()
        return power * 4

    lax.fori_loop(0, OTHERS, drain_mate, jnp.int32(1))
    for way in range(2):
        along_y(way, 0, 0, whole).wait_send()
        along_y(way, 1, 0, halves[way]).wait_send()
        for lane_y in range(4):
            for distance in range(4):
                along_z(way, lane_y, distance, halves[way] if distance == 3 else whole).wait_send()
    mate_stats(functools.partial(wait_mate, received=False))

    def drain_ring(chunk, carry):
        for step in range(3):
            for way in range(2):
                ring(step, way, chunk).wait_send()
        return carry

    lax.fori_loop(0, chunks, drain_ring, 0)


def on_device(
    hidden, final_gain, key_weight, value_weight, queries, context_grad, passage_count, passage_slot, slot_question
):
    slots_here, seq_len, width = hidden.shape
    questions, most = passage_slot.shape
    tensor_ways = lax.axis_size("mp")
    token_share = seq_len // tensor_ways
    inner = key_weight.shape[1]
    me = lax.axis_index("segment") * lax.axis_size("dp") + lax.axis_index("dp")
    my_slots = me * slots_here + jnp.arange(slots_here, dtype=jnp.int32)
    question_ids = jnp.arange(questions, dtype=jnp.int32)
    present = (passage_slot >= 0) & (jnp.arange(most, dtype=jnp.int32)[None, :] < passage_count[:, None])
    matched = (passage_slot[None] == my_slots[:, None, None]) & present[None]
    question = jnp.max(jnp.where(matched, question_ids[None, :, None], -1), axis=(1, 2))
    row = jnp.sum(jnp.where(slot_question[None, :] == question[:, None], question_ids[None, :], 0), axis=1)
    owner = jnp.concatenate([question, row])
    slots = jnp.where(present, passage_slot, passage_slot[:, :1]).reshape(-1)
    rows = slots_here * seq_len
    chunks = 4
    rows_half = slots_here * token_share // 2
    smem, anywhere, vmem = (
        pl.BlockSpec(memory_space=pltpu.SMEM),
        pl.BlockSpec(memory_space=pl.ANY),
        pl.BlockSpec(memory_space=pltpu.VMEM),
    )
    half, single, dma = jnp.bfloat16, jnp.float32, pltpu.SemaphoreType.DMA
    shape_of = (2, 128, inner)
    return pl.pallas_call(
        reader_kernel,
        out_shape=jax.ShapeDtypeStruct((slots_here, token_share, width), half),
        in_specs=[smem, smem, smem, vmem] + [anywhere] * 5,
        out_specs=vmem,
        scratch_shapes=[
            pltpu.VMEM((2, 2, 32, 128, inner), half),
            pltpu.VMEM((slots_here, tensor_ways, token_share, width), half),
            pltpu.VMEM((16, rows, 256), half),
            pltpu.VMEM((2, rows, inner), single),
            pltpu.VMEM((2, slots_here, seq_len, inner), half),
            pltpu.VMEM((slots_here, inner // 128, 128, 128), single),
            pltpu.VMEM((slots_here, inner // 128, 128, 128), single),
            pltpu.VMEM((64, slots_here, 16, 128), half),
            pltpu.VMEM((tensor_ways, slots_here * token_share, 2 * inner), half),
            pltpu.VMEM((3, 2, chunks, rows_half, width // chunks), half),
            pltpu.VMEM((3, 2, chunks, rows_half, width // chunks), half),
            pltpu.VMEM((chunks, 2 * rows_half, width // chunks), single),
            dma((5,)),
            dma((2, 2, 3)),
            dma((2, 4, 2, 3)),
            dma((2, 32)),
            dma((2, 32)),
            dma((2, 32)),
            dma((2, 2)),
            dma((2, 2)),
            dma((2, 4, 4)),
            dma((2, 4, 4)),
            dma((32, 2)),
            dma((32, 2)),
            dma((3, 2, chunks)),
            dma((3, 2, chunks)),
        ],
        compiler_params=pltpu.CompilerParams(collective_id=0, has_side_effects=True, vmem_limit_bytes=60 << 20),
    )(
        owner,
        passage_count,
        slots,
        final_gain.astype(single)[None],
        hidden.reshape(slots_here, tensor_ways, token_share, width),
        key_weight.reshape(shape_of),
        value_weight.reshape(shape_of),
        queries,
        context_grad,
    )


def solution(mesh):
    in_specs = (
        P(("segment", "dp"), None, None),
        P(),
        P("dp", "mp"),
        P("dp", "mp"),
        P("dp", None, "mp"),
        P("dp", None, "mp"),
        P(),
        P(),
        P(),
    )
    return jax.shard_map(
        on_device, mesh=mesh, in_specs=in_specs, out_specs=P(("segment", "dp"), "mp", None), check_vma=False
    )
```

```python
import functools
import math

import jax
import jax.numpy as jnp
from jax import lax
from jax.experimental import pallas as pl
from jax.experimental.pallas import tpu as pltpu
from jax.sharding import PartitionSpec as P

HEAD_DIM = 64
EPSILON = 1e-06
TINY = 1.2e-38
MESH = pl.DeviceIdType.MESH

ARRIVAL = (
    (3, 0), (1, 0), (0, 3), (0, 1), (2, 0), (3, 3), (3, 1), (1, 3), (1, 1), (0, 2), (2, 3), (2, 1), (3, 2), (1, 2), (2, 2),
)
FIRST_TABLE = sum(first * 4**k for k, (first, _) in enumerate(ARRIVAL))
SECOND_TABLE = sum(second * 4**k for k, (_, second) in enumerate(ARRIVAL))
OTHERS = len(ARRIVAL)
LAG = 2
NORM_STEPS = 8


def reader_kernel(
    counts, slots, slot_table, count_table, row_table, gain_half, hidden_hbm, key_shard, value_shard, query_shard, grad_shard,
    out,
    owner, gain, blocks, states, normed, total, kv_rows, score_buf, prob_grad_buf, stats, grad_rows, send_buf, recv_buf, sum_buf,
    local_sem, first_send, second_send, mate_send, block_recv, mate_recv,
    stat_send_y, stat_recv_y, stat_send_z, stat_recv_z, stat_send_mate, stat_recv_mate,
    ring_send, ring_recv,
):
    segment, column, x = lax.axis_index("segment"), lax.axis_index("dp"), lax.axis_index("mp")
    z_hi, core = lax.div(segment, 2), lax.rem(segment, 2)
    z_lo, y = lax.div(column, 4), lax.rem(column, 4)
    z_next, z_prev = lax.rem(z_lo + 1, 4), lax.rem(z_lo + 3, 4)
    flip_next, flip_prev = lax.div(z_lo + 1, 4), 1 - lax.div(z_lo + 3, 4)
    y_up = (segment, z_lo * 4 + lax.rem(y + 1, 4), x)
    y_down = (segment, z_lo * 4 + lax.rem(y + 3, 4), x)
    z_up = (lax.rem(z_hi + flip_next, 2) * 2 + core, z_next * 4 + y, x)
    z_down = (lax.rem(z_hi + flip_prev, 2) * 2 + core, z_prev * 4 + y, x)
    mate = (z_hi * 2 + 1 - core, column, x)
    x_up = (segment, column, lax.rem(x + 1, 4))
    x_down = (segment, column, lax.rem(x + 3, 4))

    def by_core(if_zero, if_one):
        return tuple(a * (1 - core) + b * core for a, b in zip(if_zero, if_one))

    first_up, first_down = by_core(y_up, z_up), by_core(y_down, z_down)
    second_up, second_down = by_core(z_up, y_up), by_core(z_down, y_down)
    first_at = y * (1 - core) + z_lo * core
    second_at = z_lo * (1 - core) + y * core
    first_stride, second_stride = 1 + 3 * core, 4 - 3 * core
    other = 1 - core

    def remote(src, dst, send, recv, device):
        return pltpu.make_async_remote_copy(
            src_ref=src, dst_ref=dst, send_sem=send, recv_sem=recv, device_id=device, device_id_type=MESH
        )

    mine = pl.ds(2 * column, 2)
    local_copies = [
        pltpu.make_async_copy(src, dst, local_sem.at[k])
        for k, (src, dst) in enumerate(
            (
                (key_shard, blocks.at[0, 0, mine]),
                (value_shard, blocks.at[0, 1, mine]),
                (query_shard, blocks.at[1, 0, mine]),
                (grad_shard, blocks.at[1, 1, mine]),
                (hidden_hbm, states),
            )
        )
    ]
    for copy in local_copies:
        copy.start()
    barrier = pltpu.get_barrier_semaphore()
    for device in (y_up, y_down, z_up, z_down, mate, x_up, x_down):
        pl.semaphore_signal(barrier, inc=1, device_id=device, device_id_type=MESH)
    pl.semaphore_wait(barrier, 7)
    for copy in local_copies[:4]:
        copy.wait()

    def block_copy(kind, index, send, recv, device):
        ref = blocks.at[kind, core, index]
        return remote(ref, ref, send, recv, device)

    def to_first(kind, way, which, index):
        return block_copy(
            kind, index, first_send.at[kind, way, which], block_recv.at[kind, index], (first_up, first_down)[way]
        )

    def to_second(kind, lane, way, which, index):
        return block_copy(
            kind, index, second_send.at[kind, lane, way, which], block_recv.at[kind, index],
            (second_up, second_down)[way],
        )

    def to_mate(kind, index):
        return block_copy(kind, index, mate_send.at[kind, index], mate_recv.at[kind, index], mate)

    def send_own(kind):
        for half in range(2):
            for way in range(2):
                to_first(kind, way, half, 2 * column + half).start()
        for half in range(2):
            for way in range(2):
                to_second(kind, 0, way, half, 2 * column + half).start()

    send_own(0)
    local_copies[4].wait()

    slots_here = states.shape[0]
    width = states.shape[-1]
    parts = states.shape[1]
    token_share = states.shape[2]

    gain_rows = gain_half[...].astype(jnp.float32)
    for k in range(gain_rows.shape[0]):
        gain[:, k * 128 : k * 128 + 128] = gain_rows[k : k + 1]

    def norm_rows(step):
        slot, part = lax.div(step, parts), lax.rem(step, parts)
        rows = states[slot, part].astype(jnp.float32)
        inv = lax.rsqrt(jnp.mean(rows * rows, axis=-1, keepdims=True) + EPSILON)
        scaled = (rows * inv * gain[...]).astype(jnp.bfloat16)
        at = pl.ds(pl.multiple_of(step * token_share, token_share), token_share)
        for shard in range(16):
            normed[shard, at, :] = scaled[:, shard * 256 : shard * 256 + 256]

    me = segment * 16 + column
    question_ids = lax.broadcasted_iota(jnp.int32, slot_table.shape, 1)
    passage_ids = lax.broadcasted_iota(jnp.int32, slot_table.shape, 0)
    row_ids = lax.broadcasted_iota(jnp.int32, row_table.shape, 1)

    def find_owner(slot):
        found = (slot_table[...] == me * slots_here + slot) & (passage_ids < count_table[...])
        question = jnp.max(jnp.where(found, question_ids, -1))
        owner[slot] = question
        owner[slots_here + slot] = jnp.max(jnp.where(row_table[...] == question, row_ids, 0))

    def project(which, shard, first):
        weight = blocks[0, which, pl.ds(2 * shard, 2)].reshape(256, blocks.shape[-1])
        product = jnp.dot(normed[shard], weight, preferred_element_type=jnp.float32)
        total[which] = product if first else total[which] + product

    def table(power, first_base, second_base, stride_first, stride_second):
        first, second = lax.rem(lax.div(FIRST_TABLE, power), 4), lax.rem(lax.div(SECOND_TABLE, power), 4)
        shard = lax.rem(first_base + first, 4) * stride_first + lax.rem(second_base + second, 4) * stride_second
        return first, second, shard

    def next_power(power, k):
        return jnp.where(k == OTHERS - 1, 1, power * 4)

    def own_table(power):
        return table(power, first_at, second_at, first_stride, second_stride)

    def mate_table(power):
        return table(power, second_at, first_at, second_stride, first_stride)

    def advance(power, done):
        return jnp.where(done >= 0, next_power(power, lax.rem(jnp.maximum(done, 0), OTHERS)), power)

    def gather_step(step, powers):
        kind = lax.div(step, OTHERS)
        arrived, ready, mate_ready = step - LAG, step - NORM_STEPS, step - NORM_STEPS - LAG

        @pl.when(step < 2 * OTHERS)
        def _():
            first, second, shard = own_table(powers[0])
            for half in range(2):
                index = 2 * shard + half
                to_first(kind, 0, 0, index).wait_recv()

                @pl.when((second == 0) & (first == (3 if half == 0 else 1)))
                def _():
                    to_first(kind, half, 2, index).start()

                @pl.when(second == 0)
                def _():
                    to_second(kind, first, 0, half, index).start()
                    to_second(kind, first, 1, half, index).start()

                @pl.when(second == (3 if half == 0 else 1))
                def _():
                    to_second(kind, first, half, 2, index).start()

                to_mate(kind, index).start()

        @pl.when(step == OTHERS - 6)
        def _():
            send_own(1)

        @pl.when(arrived >= 0)
        def _():
            mate_kind = lax.div(arrived, OTHERS)
            _, _, shard = mate_table(powers[1])
            for half in range(2):
                ref = blocks.at[mate_kind, other, 2 * shard + half]
                remote(
                    ref, ref, mate_send.at[mate_kind, 2 * shard + half], mate_recv.at[mate_kind, 2 * shard + half], mate
                ).wait_recv()

        @pl.when(step < NORM_STEPS)
        def _():
            each = slots_here * parts // NORM_STEPS
            for k in range(each):
                norm_rows(step * each + k)

        @pl.when(step < slots_here)
        def _():
            find_owner(step)

        @pl.when(ready == 0)
        def _():
            project(0, column, True)
            project(1, column, True)

        @pl.when((ready >= 0) & (ready < OTHERS))
        def _():
            project(core, own_table(powers[2])[2], False)

        @pl.when((mate_ready >= 0) & (mate_ready < OTHERS))
        def _():
            project(other, mate_table(powers[3])[2], False)

        return tuple(advance(power, done) for power, done in zip(powers, (step, arrived, ready, mate_ready)))

    lax.fori_loop(0, 2 * OTHERS + LAG, gather_step, (jnp.int32(1),) * 4)

    for which in range(2):
        for slot in range(slots_here):
            kv_rows[which, slot] = total[which, slot * 64 : slot * 64 + 64, :].astype(jnp.bfloat16)

    lane = lax.broadcasted_iota(jnp.int32, (64, 128), 1)
    left = lane < HEAD_DIM
    left_half = left.astype(jnp.float32).astype(jnp.bfloat16)
    right_half = (1.0 - left.astype(jnp.float32)).astype(jnp.bfloat16)
    pairs = kv_rows.shape[-1] // 128
    scaling = 1.0 / math.sqrt(HEAD_DIM)
    across = (((1,), (1,)), ((), ()))

    def both_heads(top, bottom):
        return jnp.concatenate([jnp.broadcast_to(top, (64, 128)), jnp.broadcast_to(bottom, (64, 128))], axis=0)

    def scores_of(slot, carry):
        row = owner[slots_here + slot]
        sums, deltas = [], []
        for pair in range(pairs):
            cols = slice(pair * 128, pair * 128 + 128)
            keys, values = kv_rows[0, slot, :, cols], kv_rows[1, slot, :, cols]
            key_pair = jnp.concatenate([keys * left_half, keys * right_half], axis=0)
            value_pair = jnp.concatenate([values * left_half, values * right_half], axis=0)
            queries = blocks[1, 0, row, :, cols]
            grads = blocks[1, 1, row, :, cols]
            scores = lax.dot_general(key_pair, queries, across, preferred_element_type=jnp.float32) * scaling
            prob_grads = lax.dot_general(value_pair, grads, across, preferred_element_type=jnp.float32)
            score_buf[slot, pair] = scores
            prob_grad_buf[slot, pair] = prob_grads
            weights = jnp.exp(scores)
            both = [jnp.sum(weights[k * 64 : k * 64 + 64], axis=0, keepdims=True) for k in range(2)]
            log_both = both_heads(*[jnp.log(jnp.maximum(b, TINY)) for b in both])
            moved = jnp.exp(scores - log_both) * prob_grads
            sums += both
            deltas += [jnp.sum(moved[k * 64 : k * 64 + 64], axis=0, keepdims=True) for k in range(2)]
        stats[me, slot] = jnp.concatenate(sums + deltas, axis=0).astype(jnp.bfloat16)
        return carry

    lax.fori_loop(0, slots_here, scores_of, 0)

    z = z_hi * 4 + z_lo
    half_slots = slots_here // 2
    halves = (pl.ds(0, half_slots), pl.ds(half_slots, half_slots))
    whole = pl.ds(0, slots_here)

    def piece(z_of, y_of, core_of):
        return (lax.div(z_of, 4) * 2 + core_of) * 16 + lax.rem(z_of, 4) * 4 + y_of

    def stat_copy(at, part, send, recv, device):
        ref = stats.at[at, part]
        return remote(ref, ref, send, recv, device)

    def y_piece(offset):
        return piece(z, lax.rem(y + offset, 4), core)

    def along_y(way, which, offset, part):
        return stat_copy(
            y_piece(offset), part, stat_send_y.at[way, which], stat_recv_y.at[way, which], (y_up, y_down)[way]
        )

    def share(z_of, y_of, part, which):
        at = piece(z_of, y_of, core)
        return stat_copy(
            at, part, stat_send_mate.at[z_of * 4 + y_of, which], stat_recv_mate.at[z_of * 4 + y_of, which], mate
        )

    def along_z(way, lane_y, distance, part):
        z_of = lax.rem(z + (8 - distance if way == 0 else distance), 8)
        at = piece(z_of, lax.rem(y + lane_y, 4), core)
        return stat_copy(
            at, part, stat_send_z.at[way, lane_y, distance], stat_recv_z.at[way, lane_y, distance],
            (z_up, z_down)[way],
        )

    along_y(0, 0, 0, whole).start()
    along_y(1, 0, 0, whole).start()
    along_z(0, 0, 0, whole).start()
    along_z(1, 0, 0, whole).start()
    share(z, y, whole, 0).start()
    for way, offset in ((0, 3), (1, 1)):
        along_y(way, 0, offset, whole).wait_recv()
        along_y(way, 1, offset, halves[way]).start()
        along_z(0, offset, 0, whole).start()
        along_z(1, offset, 0, whole).start()
        share(z, lax.rem(y + offset, 4), whole, 0).start()
    for way in range(2):
        along_y(way, 1, 2, halves[way]).wait_recv()
    along_z(0, 2, 0, whole).start()
    along_z(1, 2, 0, whole).start()
    share(z, lax.rem(y + 2, 4), whole, 0).start()
    for distance in (1, 2, 3, 4):
        for lane_y in (0, 3, 1, 2):
            y_of = lax.rem(y + lane_y, 4)
            for way in range(2):
                z_of = lax.rem(z + (8 - distance if way == 0 else distance), 8)
                along_z(way, lane_y, distance - 1, halves[way] if distance == 4 else whole).wait_recv()
                if distance < 4:
                    along_z(way, lane_y, distance, halves[way] if distance == 3 else whole).start()
                    share(z_of, y_of, whole, 0).start()
                else:
                    share(z_of, y_of, halves[way], way).start()

    def mate_stats(fn):
        def step(k, carry):
            z_of, y_of = lax.div(k, 4), lax.rem(k, 4)
            fn(z_of, y_of)
            return carry

        lax.fori_loop(0, 32, step, 0)

    def wait_mate(z_of, y_of, received):
        far = lax.rem(z_of - z + 8, 8) == 4

        def finish(copy):
            copy.wait_recv() if received else copy.wait_send()

        @pl.when(far)
        def _():
            for way in range(2):
                finish(share(z_of, y_of, halves[way], way))

        @pl.when(jnp.logical_not(far))
        def _():
            finish(share(z_of, y_of, whole, 0))

    mate_stats(functools.partial(wait_mate, received=True))

    def grads_of(slot, carry):
        question = owner[slot]
        row = owner[slots_here + slot]
        holds = question >= 0
        base = jnp.maximum(question, 0)
        count = counts[base]
        tiles = []
        for k in range(16):
            at = slots[jnp.where(k < count, k, 0), base]
            tile = stats[lax.div(at, slots_here), lax.rem(at, slots_here)].astype(jnp.float32)
            tiles.append((tile[:8], tile[8:], k < count))
        zero = jnp.zeros((8, 128), jnp.float32)
        all_sum = zero
        for sums, _, live in tiles:
            all_sum = all_sum + jnp.where(live, sums, zero)
        log_sum = jnp.log(jnp.maximum(all_sum, TINY))
        delta = zero
        for sums, deltas, live in tiles:
            share_of = jnp.exp(jnp.log(jnp.maximum(sums, TINY)) - log_sum)
            delta = delta + jnp.where(live, share_of * deltas, zero)
        at = pl.ds(pl.multiple_of(slot * token_share, token_share), token_share)
        inner = kv_rows.shape[-1]
        for pair in range(pairs):
            cols = slice(pair * 128, pair * 128 + 128)
            heads = [2 * pair, 2 * pair + 1]
            log_both = both_heads(*[log_sum[h : h + 1] for h in heads])
            delta_both = both_heads(*[delta[h : h + 1] for h in heads])
            probs = jnp.exp(score_buf[slot, pair] - log_both)
            score_grads = (probs * (prob_grad_buf[slot, pair] - delta_both)).astype(jnp.bfloat16)
            queries = blocks[1, 0, row, :, cols]
            grads = blocks[1, 1, row, :, cols]
            key_grads = jnp.dot(score_grads, queries, preferred_element_type=jnp.float32) * scaling
            value_grads = jnp.dot(probs.astype(jnp.bfloat16), grads, preferred_element_type=jnp.float32)
            for offset, both in ((0, key_grads), (inner, value_grads)):
                merged = jnp.where(left, both[:64], both[64:])
                merged = jnp.where(holds, merged, jnp.zeros_like(merged)).astype(jnp.bfloat16)
                for part in range(parts):
                    grad_rows[part, at, offset + pair * 128 : offset + pair * 128 + 128] = merged[
                        part * token_share : part * token_share + token_share
                    ]
        return carry

    lax.fori_loop(0, slots_here, grads_of, 0)

    rows_half = slots_here * token_share // 2
    chunks = recv_buf.shape[2]
    chunk_width = recv_buf.shape[-1]
    tiles_here = chunk_width // 256

    def lhs(first, second):
        return jnp.concatenate([grad_rows[first], grad_rows[second]], axis=0)

    def back(rows, chunk, tile):
        index = pl.ds(2 * (chunk * tiles_here + tile), 2)
        inner = kv_rows.shape[-1]
        keys = blocks[0, 0, index].reshape(256, inner)
        values = blocks[0, 1, index].reshape(256, inner)
        return lax.dot_general(rows[:, :inner], keys, across, preferred_element_type=jnp.float32) + lax.dot_general(
            rows[:, inner:], values, across, preferred_element_type=jnp.float32
        )

    def ring(step, way, chunk):
        return remote(
            send_buf.at[step, way, chunk], recv_buf.at[step, way, chunk],
            ring_send.at[step, way, chunk], ring_recv.at[step, way, chunk], (x_up, x_down)[way],
        )

    def first_chunk(chunk, carry):
        rows = lhs(lax.rem(x + 3, 4), lax.rem(x + 1, 4))
        for tile in range(tiles_here):
            cols = slice(tile * 256, tile * 256 + 256)
            product = back(rows, chunk, tile).astype(jnp.bfloat16)
            send_buf[0, 0, chunk, :, cols] = product[:rows_half]
            send_buf[2, 1, chunk, :, cols] = product[rows_half : 2 * rows_half]
            send_buf[2, 0, chunk, :, cols] = product[2 * rows_half : 3 * rows_half]
            send_buf[0, 1, chunk, :, cols] = product[3 * rows_half :]
        ring(0, 0, chunk).start()
        ring(0, 1, chunk).start()
        return carry

    lax.fori_loop(0, chunks, first_chunk, 0)

    def pass_on(step, chunk):
        for way in range(2):
            ring(step - 1, way, chunk).wait_recv()
            send_buf[step, way, chunk] = (
                send_buf[step, way, chunk].astype(jnp.float32) + recv_buf[step - 1, way, chunk].astype(jnp.float32)
            ).astype(jnp.bfloat16)
            ring(step, way, chunk).start()

    def second_chunk(chunk, carry):
        rows = lhs(lax.rem(x + 2, 4), x)
        for tile in range(tiles_here):
            cols = slice(tile * 256, tile * 256 + 256)
            product = back(rows, chunk, tile).astype(jnp.bfloat16)
            send_buf[1, 0, chunk, :, cols] = product[:rows_half]
            send_buf[1, 1, chunk, :, cols] = product[rows_half : 2 * rows_half]
            sum_buf[chunk, :, cols] = product[2 * rows_half :].astype(jnp.float32)
        pass_on(1, chunk)
        return carry

    lax.fori_loop(0, chunks, second_chunk, 0)

    def third_chunk(chunk, carry):
        pass_on(2, chunk)
        return carry

    lax.fori_loop(0, chunks, third_chunk, 0)

    def last_chunk(chunk, carry):
        for way in range(2):
            ring(2, way, chunk).wait_recv()
            at = slice(way * rows_half, way * rows_half + rows_half)
            sum_buf[chunk, at] = sum_buf[chunk, at] + recv_buf[2, way, chunk].astype(jnp.float32)
        return carry

    lax.fori_loop(0, chunks, last_chunk, 0)

    def finish_slot(slot, carry):
        at = pl.ds(pl.multiple_of(slot * token_share, token_share), token_share)
        rows = states[slot, x].astype(jnp.float32)
        inv = lax.rsqrt(jnp.mean(rows * rows, axis=-1, keepdims=True) + EPSILON)
        scaled = gain[...] * jnp.concatenate([sum_buf[c, at, :] for c in range(chunks)], axis=-1)
        mean = jnp.mean(rows * scaled, axis=-1, keepdims=True)
        out[slot] = (inv * scaled - rows * (inv * inv * inv) * mean).astype(jnp.bfloat16)
        return carry

    lax.fori_loop(0, slots_here, finish_slot, 0)

    for kind in range(2):
        for way in range(2):
            for which in range(3):
                to_first(kind, way, which, 2 * column).wait_send()

    def drain_second(k, carry):
        for kind in range(2):
            for way in range(2):
                for which in range(3):
                    to_second(kind, k, way, which, 2 * column).wait_send()
        return carry

    lax.fori_loop(0, 4, drain_second, 0)

    def drain_mate(k, power):
        _, _, shard = table(power, first_at, second_at, first_stride, second_stride)
        for kind in range(2):
            for half in range(2):
                to_mate(kind, 2 * shard + half).wait_send()
        return power * 4

    lax.fori_loop(0, OTHERS, drain_mate, jnp.int32(1))
    for way in range(2):
        along_y(way, 0, 0, whole).wait_send()
        along_y(way, 1, 0, halves[way]).wait_send()
        for lane_y in range(4):
            for distance in range(4):
                along_z(way, lane_y, distance, halves[way] if distance == 3 else whole).wait_send()
    mate_stats(functools.partial(wait_mate, received=False))

    def drain_ring(chunk, carry):
        for step in range(3):
            for way in range(2):
                ring(step, way, chunk).wait_send()
        return carry

    lax.fori_loop(0, chunks, drain_ring, 0)


def on_device(
    hidden, final_gain, key_weight, value_weight, queries, context_grad, passage_count, passage_slot, slot_question
):
    slots_here, seq_len, width = hidden.shape
    tensor_ways = lax.axis_size("mp")
    token_share = seq_len // tensor_ways
    inner = key_weight.shape[1]
    slots = passage_slot.T
    rows = slots_here * seq_len
    chunks = 4
    rows_half = slots_here * token_share // 2
    smem, anywhere, vmem = (
        pl.BlockSpec(memory_space=pltpu.SMEM),
        pl.BlockSpec(memory_space=pl.ANY),
        pl.BlockSpec(memory_space=pltpu.VMEM),
    )
    half, single, dma = jnp.bfloat16, jnp.float32, pltpu.SemaphoreType.DMA
    shape_of = (2, 128, inner)
    return pl.pallas_call(
        reader_kernel,
        out_shape=pltpu.VMEM((slots_here, token_share, width), half),
        in_specs=[smem, smem] + [vmem] * 4 + [anywhere] * 5,
        out_specs=vmem,
        scratch_shapes=[
            pltpu.SMEM((2 * slots_here,), jnp.int32),
            pltpu.VMEM((1, width), single),
            pltpu.VMEM((2, 2, 32, 128, inner), half),
            pltpu.VMEM((slots_here, tensor_ways, token_share, width), half),
            pltpu.VMEM((16, rows, 256), half),
            pltpu.VMEM((2, rows, inner), single),
            pltpu.VMEM((2, slots_here, seq_len, inner), half),
            pltpu.VMEM((slots_here, inner // 128, 128, 128), single),
            pltpu.VMEM((slots_here, inner // 128, 128, 128), single),
            pltpu.VMEM((64, slots_here, 16, 128), half),
            pltpu.VMEM((tensor_ways, slots_here * token_share, 2 * inner), half),
            pltpu.VMEM((3, 2, chunks, rows_half, width // chunks), half),
            pltpu.VMEM((3, 2, chunks, rows_half, width // chunks), half),
            pltpu.VMEM((chunks, 2 * rows_half, width // chunks), single),
            dma((5,)),
            dma((2, 2, 3)),
            dma((2, 4, 2, 3)),
            dma((2, 32)),
            dma((2, 32)),
            dma((2, 32)),
            dma((2, 2)),
            dma((2, 2)),
            dma((2, 4, 4)),
            dma((2, 4, 4)),
            dma((32, 2)),
            dma((32, 2)),
            dma((3, 2, chunks)),
            dma((3, 2, chunks)),
        ],
        compiler_params=pltpu.CompilerParams(collective_id=0, has_side_effects=True, vmem_limit_bytes=60 << 20),
    )(
        passage_count,
        slots,
        slots,
        passage_count[None],
        slot_question[None],
        final_gain.reshape(-1, 128),
        hidden.reshape(slots_here, tensor_ways, token_share, width),
        key_weight.reshape(shape_of),
        value_weight.reshape(shape_of),
        queries,
        context_grad,
    )


def solution(mesh):
    in_specs = (
        P(("segment", "dp"), None, None),
        P(),
        P("dp", "mp"),
        P("dp", "mp"),
        P("dp", None, "mp"),
        P("dp", None, "mp"),
        P(),
        P(),
        P(),
    )
    return jax.shard_map(
        on_device, mesh=mesh, in_specs=in_specs, out_specs=P(("segment", "dp"), "mp", None), check_vma=False
    )
```

```python
import math

import jax
import jax.numpy as jnp
from jax import lax
from jax.experimental import pallas as pl
from jax.experimental.pallas import tpu as pltpu
from jax.sharding import PartitionSpec as P

HEAD_DIM = 64
EPSILON = 1e-06
TINY = 1.2e-38
MESH = pl.DeviceIdType.MESH

ARRIVAL = (
    (3, 0), (1, 0), (0, 3), (0, 1), (2, 0), (3, 3), (3, 1), (1, 3), (1, 1), (0, 2), (2, 3), (2, 1), (3, 2), (1, 2), (2, 2),
)
FIRST_TABLE = sum(first * 4**k for k, (first, _) in enumerate(ARRIVAL))
SECOND_TABLE = sum(second * 4**k for k, (_, second) in enumerate(ARRIVAL))
OTHERS = len(ARRIVAL)
LAG = 2
NORM_STEPS = 8


def reader_kernel(
    counts, slots, slot_table, count_table, row_table, gain_half, hidden_hbm, key_shard, value_shard, query_shard, grad_shard,
    out,
    owner, gain, blocks, states, normed, total, kv_rows, score_buf, prob_grad_buf, stats, grad_rows, send_buf, recv_buf, sum_buf,
    local_sem, block_send, mate_send, block_recv, mate_recv,
    stat_send, stat_recv_z, stat_recv_y, stat_recv_far, stat_recv_mate,
    ring_send, ring_recv,
):
    segment, column, x = lax.axis_index("segment"), lax.axis_index("dp"), lax.axis_index("mp")
    z_hi, core = lax.div(segment, 2), lax.rem(segment, 2)
    z_lo, y = lax.div(column, 4), lax.rem(column, 4)
    z_next, z_prev = lax.rem(z_lo + 1, 4), lax.rem(z_lo + 3, 4)
    flip_next, flip_prev = lax.div(z_lo + 1, 4), 1 - lax.div(z_lo + 3, 4)
    y_up = (segment, z_lo * 4 + lax.rem(y + 1, 4), x)
    y_down = (segment, z_lo * 4 + lax.rem(y + 3, 4), x)
    z_up = (lax.rem(z_hi + flip_next, 2) * 2 + core, z_next * 4 + y, x)
    z_down = (lax.rem(z_hi + flip_prev, 2) * 2 + core, z_prev * 4 + y, x)
    mate = (z_hi * 2 + 1 - core, column, x)
    x_up = (segment, column, lax.rem(x + 1, 4))
    x_down = (segment, column, lax.rem(x + 3, 4))

    z = z_hi * 4 + z_lo

    def z_peer(z_of):
        return (lax.div(z_of, 4) * 2 + core, lax.rem(z_of, 4) * 4 + y, x)

    def by_core(if_zero, if_one):
        return tuple(a * (1 - core) + b * core for a, b in zip(if_zero, if_one))

    first_up, first_down = by_core(y_up, z_up), by_core(y_down, z_down)
    second_up, second_down = by_core(z_up, y_up), by_core(z_down, y_down)
    first_at = y * (1 - core) + z_lo * core
    second_at = z_lo * (1 - core) + y * core
    first_stride, second_stride = 1 + 3 * core, 4 - 3 * core
    other = 1 - core

    def remote(src, dst, send, recv, device):
        return pltpu.make_async_remote_copy(
            src_ref=src, dst_ref=dst, send_sem=send, recv_sem=recv, device_id=device, device_id_type=MESH
        )

    mine = pl.ds(2 * column, 2)
    local_copies = [
        pltpu.make_async_copy(src, dst, local_sem.at[k])
        for k, (src, dst) in enumerate(
            (
                (key_shard, blocks.at[0, 0, mine]),
                (value_shard, blocks.at[0, 1, mine]),
                (query_shard, blocks.at[1, 0, mine]),
                (grad_shard, blocks.at[1, 1, mine]),
                (hidden_hbm, states),
            )
        )
    ]
    for copy in local_copies:
        copy.start()
    barrier = pltpu.get_barrier_semaphore()
    for device in [y_up, y_down, mate, x_up, x_down] + [z_peer(lax.rem(z + d, 8)) for d in range(1, 8)]:
        pl.semaphore_signal(barrier, inc=1, device_id=device, device_id_type=MESH)
    pl.semaphore_wait(barrier, 12)
    for copy in local_copies[:4]:
        copy.wait()

    def block_copy(kind, index, send, recv, device):
        ref = blocks.at[kind, core, index]
        return remote(ref, ref, send, recv, device)

    def to_first(kind, way, index):
        return block_copy(kind, index, block_send.at[kind], block_recv.at[kind, index], (first_up, first_down)[way])

    def to_second(kind, way, index):
        return block_copy(kind, index, block_send.at[kind], block_recv.at[kind, index], (second_up, second_down)[way])

    def to_mate(kind, index):
        return block_copy(kind, index, mate_send.at[kind], mate_recv.at[kind, lax.div(index, 2)], mate)

    def send_own(kind):
        for half in range(2):
            for way in range(2):
                to_first(kind, way, 2 * column + half).start()
        for half in range(2):
            for way in range(2):
                to_second(kind, way, 2 * column + half).start()

    send_own(0)
    local_copies[4].wait()

    slots_here = states.shape[0]
    width = states.shape[-1]
    parts = states.shape[1]
    token_share = states.shape[2]

    gain_rows = gain_half[...].astype(jnp.float32)
    for k in range(gain_rows.shape[0]):
        gain[:, k * 128 : k * 128 + 128] = gain_rows[k : k + 1]

    def norm_rows(step):
        slot, part = lax.div(step, parts), lax.rem(step, parts)
        rows = states[slot, part].astype(jnp.float32)
        inv = lax.rsqrt(jnp.mean(rows * rows, axis=-1, keepdims=True) + EPSILON)
        scaled = (rows * inv * gain[...]).astype(jnp.bfloat16)
        at = pl.ds(pl.multiple_of(step * token_share, token_share), token_share)
        for shard in range(16):
            normed[shard, at, :] = scaled[:, shard * 256 : shard * 256 + 256]

    me = segment * 16 + column
    question_ids = lax.broadcasted_iota(jnp.int32, slot_table.shape, 1)
    passage_ids = lax.broadcasted_iota(jnp.int32, slot_table.shape, 0)
    row_ids = lax.broadcasted_iota(jnp.int32, row_table.shape, 1)

    def find_owner(slot):
        found = (slot_table[...] == me * slots_here + slot) & (passage_ids < count_table[...])
        question = jnp.max(jnp.where(found, question_ids, -1))
        owner[slot] = question
        owner[slots_here + slot] = jnp.max(jnp.where(row_table[...] == question, row_ids, 0))

    def project(which, shard, first):
        weight = blocks[0, which, pl.ds(2 * shard, 2)].reshape(256, blocks.shape[-1])
        product = jnp.dot(normed[shard], weight, preferred_element_type=jnp.float32)
        total[which] = product if first else total[which] + product

    def table(power, first_base, second_base, stride_first, stride_second):
        first, second = lax.rem(lax.div(FIRST_TABLE, power), 4), lax.rem(lax.div(SECOND_TABLE, power), 4)
        shard = lax.rem(first_base + first, 4) * stride_first + lax.rem(second_base + second, 4) * stride_second
        return first, second, shard

    def next_power(power, k):
        return jnp.where(k == OTHERS - 1, 1, power * 4)

    def own_table(power):
        return table(power, first_at, second_at, first_stride, second_stride)

    def mate_table(power):
        return table(power, second_at, first_at, second_stride, first_stride)

    def advance(power, done):
        return jnp.where(done >= 0, next_power(power, lax.rem(jnp.maximum(done, 0), OTHERS)), power)

    def gather_step(step, powers):
        kind = lax.div(step, OTHERS)
        arrived, ready, mate_ready = step - LAG, step - NORM_STEPS, step - NORM_STEPS - LAG

        @pl.when(step < 2 * OTHERS)
        def _():
            first, second, shard = own_table(powers[0])
            for half in range(2):
                index = 2 * shard + half
                to_first(kind, 0, index).wait_recv()

                @pl.when((second == 0) & (first == (3 if half == 0 else 1)))
                def _():
                    to_first(kind, half, index).start()

                @pl.when(second == 0)
                def _():
                    to_second(kind, 0, index).start()
                    to_second(kind, 1, index).start()

                @pl.when(second == (3 if half == 0 else 1))
                def _():
                    to_second(kind, half, index).start()

                to_mate(kind, index).start()

        @pl.when(step == OTHERS - 6)
        def _():
            send_own(1)

        @pl.when(arrived >= 0)
        def _():
            mate_kind = lax.div(arrived, OTHERS)
            _, _, shard = mate_table(powers[1])
            ref = blocks.at[mate_kind, other, pl.ds(2 * shard, 2)]
            remote(ref, ref, mate_send.at[mate_kind], mate_recv.at[mate_kind, shard], mate).wait_recv()

        @pl.when(step < NORM_STEPS)
        def _():
            each = slots_here * parts // NORM_STEPS
            for k in range(each):
                norm_rows(step * each + k)

        @pl.when(step < slots_here)
        def _():
            find_owner(step)

        @pl.when(ready == 0)
        def _():
            project(0, column, True)
            project(1, column, True)

        @pl.when((ready >= 0) & (ready < OTHERS))
        def _():
            project(core, own_table(powers[2])[2], False)

        @pl.when((mate_ready >= 0) & (mate_ready < OTHERS))
        def _():
            project(other, mate_table(powers[3])[2], False)

        return tuple(advance(power, done) for power, done in zip(powers, (step, arrived, ready, mate_ready)))

    lax.fori_loop(0, 2 * OTHERS + LAG, gather_step, (jnp.int32(1),) * 4)

    for which in range(2):
        for slot in range(slots_here):
            kv_rows[which, slot] = total[which, slot * 64 : slot * 64 + 64, :].astype(jnp.bfloat16)

    lane = lax.broadcasted_iota(jnp.int32, (64, 128), 1)
    left = lane < HEAD_DIM
    left_half = left.astype(jnp.float32).astype(jnp.bfloat16)
    right_half = (1.0 - left.astype(jnp.float32)).astype(jnp.bfloat16)
    pairs = kv_rows.shape[-1] // 128
    scaling = 1.0 / math.sqrt(HEAD_DIM)
    across = (((1,), (1,)), ((), ()))

    def both_heads(top, bottom):
        return jnp.concatenate([jnp.broadcast_to(top, (64, 128)), jnp.broadcast_to(bottom, (64, 128))], axis=0)

    def scores_of(slot, carry):
        row = owner[slots_here + slot]
        sums, deltas = [], []
        for pair in range(pairs):
            cols = slice(pair * 128, pair * 128 + 128)
            keys, values = kv_rows[0, slot, :, cols], kv_rows[1, slot, :, cols]
            key_pair = jnp.concatenate([keys * left_half, keys * right_half], axis=0)
            value_pair = jnp.concatenate([values * left_half, values * right_half], axis=0)
            queries = blocks[1, 0, row, :, cols]
            grads = blocks[1, 1, row, :, cols]
            scores = lax.dot_general(key_pair, queries, across, preferred_element_type=jnp.float32) * scaling
            prob_grads = lax.dot_general(value_pair, grads, across, preferred_element_type=jnp.float32)
            score_buf[slot, pair] = scores
            prob_grad_buf[slot, pair] = prob_grads
            weights = jnp.exp(scores)
            both = [jnp.sum(weights[k * 64 : k * 64 + 64], axis=0, keepdims=True) for k in range(2)]
            log_both = both_heads(*[jnp.log(jnp.maximum(b, TINY)) for b in both])
            moved = jnp.exp(scores - log_both) * prob_grads
            sums += both
            deltas += [jnp.sum(moved[k * 64 : k * 64 + 64], axis=0, keepdims=True) for k in range(2)]
        stats[me, slot] = jnp.concatenate(sums + deltas, axis=0).astype(jnp.bfloat16)
        return carry

    lax.fori_loop(0, slots_here, scores_of, 0)

    half_slots = slots_here // 2
    halves = (pl.ds(0, half_slots), pl.ds(half_slots, half_slots))
    whole = pl.ds(0, slots_here)

    def has_passages(z_of):
        return (core == 0) | (z_of < 4)

    def stat_copy(z_of, offset, part, recv, device):
        at = (lax.div(z_of, 4) * 2 + core) * 16 + lax.rem(z_of, 4) * 4 + lax.rem(y + offset, 4)
        ref = stats.at[at, part]
        return remote(ref, ref, stat_send, recv, device)

    def along_z(z_of, device):
        return stat_copy(z_of, 0, whole, stat_recv_z.at[z_of], device)

    def along_y(way, z_of):
        return stat_copy(z_of, 0, whole, stat_recv_y.at[way, z_of], (y_up, y_down)[way])

    def to_far(way, z_of):
        return stat_copy(z_of, (3, 1)[way], halves[way], stat_recv_far.at[z_of], (y_up, y_down)[way])

    def share(z_of, offset):
        return stat_copy(z_of, offset, whole, stat_recv_mate, mate)

    @pl.when(has_passages(z))
    def _():
        for distance in (4, 3, 5, 2, 6, 1, 7):
            along_z(z, z_peer(lax.rem(z + distance, 8))).start()

    order = (0, 7, 1, 6, 2, 5, 3, 4)

    def z_of_turn(turn):
        return lax.rem(z + order[turn], 8)

    for turn in range(len(order) + 2):
        if turn < len(order):
            z_new = z_of_turn(turn)

            @pl.when(has_passages(z_new))
            def _():
                if turn > 0:
                    along_z(z_new, mate).wait_recv()
                for way in range(2):
                    along_y(way, z_new).start()
                share(z_new, 0).start()

        if 0 <= turn - 1 < len(order):
            z_near = z_of_turn(turn - 1)

            @pl.when(has_passages(z_near))
            def _():
                for way in range(2):
                    stat_copy(z_near, (3, 1)[way], whole, stat_recv_y.at[way, z_near], mate).wait_recv()
                    to_far(way, z_near).start()
                    share(z_near, (3, 1)[way]).start()

        if 0 <= turn - 2 < len(order):
            z_far = z_of_turn(turn - 2)

            @pl.when(has_passages(z_far))
            def _():
                stat_copy(z_far, 2, whole, stat_recv_far.at[z_far], mate).wait_recv()
                share(z_far, 2).start()

    def all_shared(count):
        ref = stats.at[pl.ds(0, count)]
        return remote(ref, ref, stat_send, stat_recv_mate, mate)

    for core_of, count in ((0, 16), (1, 32)):

        @pl.when(core == core_of)
        def _():
            all_shared(count).wait_recv()

    def grads_of(slot, carry):
        question = owner[slot]
        row = owner[slots_here + slot]
        holds = question >= 0
        base = jnp.maximum(question, 0)
        count = counts[base]
        tiles = []
        for k in range(16):
            at = slots[jnp.where(k < count, k, 0), base]
            tile = stats[lax.div(at, slots_here), lax.rem(at, slots_here)].astype(jnp.float32)
            tiles.append((tile[:8], tile[8:], k < count))
        zero = jnp.zeros((8, 128), jnp.float32)
        all_sum = zero
        for sums, _, live in tiles:
            all_sum = all_sum + jnp.where(live, sums, zero)
        log_sum = jnp.log(jnp.maximum(all_sum, TINY))
        delta = zero
        for sums, deltas, live in tiles:
            share_of = jnp.exp(jnp.log(jnp.maximum(sums, TINY)) - log_sum)
            delta = delta + jnp.where(live, share_of * deltas, zero)
        at = pl.ds(pl.multiple_of(slot * token_share, token_share), token_share)
        inner = kv_rows.shape[-1]
        for pair in range(pairs):
            cols = slice(pair * 128, pair * 128 + 128)
            heads = [2 * pair, 2 * pair + 1]
            log_both = both_heads(*[log_sum[h : h + 1] for h in heads])
            delta_both = both_heads(*[delta[h : h + 1] for h in heads])
            probs = jnp.exp(score_buf[slot, pair] - log_both)
            score_grads = (probs * (prob_grad_buf[slot, pair] - delta_both)).astype(jnp.bfloat16)
            queries = blocks[1, 0, row, :, cols]
            grads = blocks[1, 1, row, :, cols]
            key_grads = jnp.dot(score_grads, queries, preferred_element_type=jnp.float32) * scaling
            value_grads = jnp.dot(probs.astype(jnp.bfloat16), grads, preferred_element_type=jnp.float32)
            for offset, both in ((0, key_grads), (inner, value_grads)):
                merged = jnp.where(left, both[:64], both[64:])
                merged = jnp.where(holds, merged, jnp.zeros_like(merged)).astype(jnp.bfloat16)
                for part in range(parts):
                    grad_rows[part, at, offset + pair * 128 : offset + pair * 128 + 128] = merged[
                        part * token_share : part * token_share + token_share
                    ]
        return carry

    lax.fori_loop(0, slots_here, grads_of, 0)

    rows_half = slots_here * token_share // 2
    chunks = recv_buf.shape[2]
    chunk_width = recv_buf.shape[-1]
    tiles_here = chunk_width // 256

    def lhs(first, second):
        return jnp.concatenate([grad_rows[first], grad_rows[second]], axis=0)

    def back(rows, chunk, tile):
        index = pl.ds(2 * (chunk * tiles_here + tile), 2)
        inner = kv_rows.shape[-1]
        keys = blocks[0, 0, index].reshape(256, inner)
        values = blocks[0, 1, index].reshape(256, inner)
        return lax.dot_general(rows[:, :inner], keys, across, preferred_element_type=jnp.float32) + lax.dot_general(
            rows[:, inner:], values, across, preferred_element_type=jnp.float32
        )

    def ring(step, way, chunk):
        return remote(
            send_buf.at[step, way, chunk], recv_buf.at[step, way, chunk],
            ring_send, ring_recv.at[step, way, chunk], (x_up, x_down)[way],
        )

    def first_chunk(chunk, carry):
        rows = lhs(lax.rem(x + 3, 4), lax.rem(x + 1, 4))
        for tile in range(tiles_here):
            cols = slice(tile * 256, tile * 256 + 256)
            product = back(rows, chunk, tile).astype(jnp.bfloat16)
            send_buf[0, 0, chunk, :, cols] = product[:rows_half]
            send_buf[2, 1, chunk, :, cols] = product[rows_half : 2 * rows_half]
            send_buf[2, 0, chunk, :, cols] = product[2 * rows_half : 3 * rows_half]
            send_buf[0, 1, chunk, :, cols] = product[3 * rows_half :]
        ring(0, 0, chunk).start()
        ring(0, 1, chunk).start()
        return carry

    lax.fori_loop(0, chunks, first_chunk, 0)

    def pass_on(step, chunk):
        for way in range(2):
            ring(step - 1, way, chunk).wait_recv()
            send_buf[step, way, chunk] = (
                send_buf[step, way, chunk].astype(jnp.float32) + recv_buf[step - 1, way, chunk].astype(jnp.float32)
            ).astype(jnp.bfloat16)
            ring(step, way, chunk).start()

    def second_chunk(chunk, carry):
        rows = lhs(lax.rem(x + 2, 4), x)
        for tile in range(tiles_here):
            cols = slice(tile * 256, tile * 256 + 256)
            product = back(rows, chunk, tile).astype(jnp.bfloat16)
            send_buf[1, 0, chunk, :, cols] = product[:rows_half]
            send_buf[1, 1, chunk, :, cols] = product[rows_half : 2 * rows_half]
            sum_buf[chunk, :, cols] = product[2 * rows_half :].astype(jnp.float32)
        pass_on(1, chunk)
        return carry

    lax.fori_loop(0, chunks, second_chunk, 0)

    def third_chunk(chunk, carry):
        pass_on(2, chunk)
        return carry

    lax.fori_loop(0, chunks, third_chunk, 0)

    def last_chunk(chunk, carry):
        for way in range(2):
            ring(2, way, chunk).wait_recv()
            at = slice(way * rows_half, way * rows_half + rows_half)
            sum_buf[chunk, at] = sum_buf[chunk, at] + recv_buf[2, way, chunk].astype(jnp.float32)
        return carry

    lax.fori_loop(0, chunks, last_chunk, 0)

    def finish_slot(slot, carry):
        at = pl.ds(pl.multiple_of(slot * token_share, token_share), token_share)
        rows = states[slot, x].astype(jnp.float32)
        inv = lax.rsqrt(jnp.mean(rows * rows, axis=-1, keepdims=True) + EPSILON)
        scaled = gain[...] * jnp.concatenate([sum_buf[c, at, :] for c in range(chunks)], axis=-1)
        mean = jnp.mean(rows * scaled, axis=-1, keepdims=True)
        out[slot] = (inv * scaled - rows * (inv * inv * inv) * mean).astype(jnp.bfloat16)
        return carry

    lax.fori_loop(0, slots_here, finish_slot, 0)

    for kind in range(2):
        ref = blocks.at[kind, core, pl.ds(0, 2 * OTHERS)]
        for sem in (block_send, mate_send):
            remote(ref, ref, sem.at[kind], block_recv.at[kind, 0], mate).wait_send()
    for alone, count in (
        (core == 0, 63),
        ((core == 1) & (z_hi == 0), 35),
        ((core == 1) & (z_hi == 1), 28),
    ):

        @pl.when(alone)
        def _():
            all_shared(count).wait_send()

    remote(send_buf, recv_buf, ring_send, ring_recv.at[0, 0, 0], x_up).wait_send()


def on_device(
    hidden, final_gain, key_weight, value_weight, queries, context_grad, passage_count, passage_slot, slot_question
):
    slots_here, seq_len, width = hidden.shape
    tensor_ways = lax.axis_size("mp")
    token_share = seq_len // tensor_ways
    inner = key_weight.shape[1]
    slots = passage_slot.T
    rows = slots_here * seq_len
    chunks = 4
    rows_half = slots_here * token_share // 2
    smem, anywhere, vmem = (
        pl.BlockSpec(memory_space=pltpu.SMEM),
        pl.BlockSpec(memory_space=pl.ANY),
        pl.BlockSpec(memory_space=pltpu.VMEM),
    )
    half, single, dma = jnp.bfloat16, jnp.float32, pltpu.SemaphoreType.DMA
    shape_of = (2, 128, inner)
    return pl.pallas_call(
        reader_kernel,
        out_shape=pltpu.VMEM((slots_here, token_share, width), half),
        in_specs=[smem, smem] + [vmem] * 4 + [anywhere] * 5,
        out_specs=vmem,
        scratch_shapes=[
            pltpu.SMEM((2 * slots_here,), jnp.int32),
            pltpu.VMEM((1, width), single),
            pltpu.VMEM((2, 2, 32, 128, inner), half),
            pltpu.VMEM((slots_here, tensor_ways, token_share, width), half),
            pltpu.VMEM((16, rows, 256), half),
            pltpu.VMEM((2, rows, inner), single),
            pltpu.VMEM((2, slots_here, seq_len, inner), half),
            pltpu.VMEM((slots_here, inner // 128, 128, 128), single),
            pltpu.VMEM((slots_here, inner // 128, 128, 128), single),
            pltpu.VMEM((64, slots_here, 16, 128), half),
            pltpu.VMEM((tensor_ways, slots_here * token_share, 2 * inner), half),
            pltpu.VMEM((3, 2, chunks, rows_half, width // chunks), half),
            pltpu.VMEM((3, 2, chunks, rows_half, width // chunks), half),
            pltpu.VMEM((chunks, 2 * rows_half, width // chunks), single),
            dma((5,)),
            dma((2,)),
            dma((2,)),
            dma((2, 32)),
            dma((2, 16)),
            dma,
            dma((8,)),
            dma((2, 8)),
            dma((8,)),
            dma,
            dma,
            dma((3, 2, chunks)),
        ],
        compiler_params=pltpu.CompilerParams(collective_id=0, has_side_effects=True, vmem_limit_bytes=60 << 20),
    )(
        passage_count,
        slots,
        slots,
        passage_count[None],
        slot_question[None],
        final_gain.reshape(-1, 128),
        hidden.reshape(slots_here, tensor_ways, token_share, width),
        key_weight.reshape(shape_of),
        value_weight.reshape(shape_of),
        queries,
        context_grad,
    )


def solution(mesh):
    in_specs = (
        P(("segment", "dp"), None, None),
        P(),
        P("dp", "mp"),
        P("dp", "mp"),
        P("dp", None, "mp"),
        P("dp", None, "mp"),
        P(),
        P(),
        P(),
    )
    return jax.shard_map(
        on_device, mesh=mesh, in_specs=in_specs, out_specs=P(("segment", "dp"), "mp", None), check_vma=False
    )
```
